32 devices in a mesh: phase: 4 (over z), slab: 4 (over y, core), coil: 2 (over x).
Axes of the slice: x: 2, y: 2, z: 4, core: 2. Of those that a mesh axis runs over, the one named last changes fastest.
Arguments:
- image: float32 [4, 4, 8, 256, 512], P('phase', None, 'slab'), may hold values from -6 to 6
- coil_maps: bfloat16 [8, 8, 256, 512], P('slab', 'coil'), may hold values from -2 to 2
- kdata: bfloat16 [256, 4, 8, 8, 512], P('phase', None, 'slab', 'coil'), may hold values from -6 to 6
- phase_bin: int32 [256, 1], P('phase'), may hold values from 0 to 3; in each aligned block of 64 rows (0 to 63, 64 to 127, ...) at most 32 rows name the same one
- line_index: int32 [256], P('phase'), may hold values from 0 to 255
Outputs:
- gradient: float32 [4, 4, 8, 256, 512], P('phase', 'coil', 'slab')
The draws below stay inside these ranges and needn't reach their ends.
Inputs may be any that keep to these rules, and one draw needn't show every extreme that they name: `phase_bin`: among the rows of one index of phase, at most 32 name the same cardiac phase, and in some device's rows one phase is named by exactly 32; every phase is named by some row.
All inputs are finite; a program needn't handle non-finite values.
Results may differ from the reference program's by a relative error of at most 0.0022.
Values may be sent and summed in bfloat16 or wider, within the bound.
No kernel may reach another device: no remote copies, remote signals or barrier semaphores. Data moves between devices by JAX's collectives and lax.ppermute only.
A program may use at most 128 MiB of HBM per device.

```python
import math
import jax
import jax.numpy as jnp
import numpy as np
from jax import lax

NX = 256
NY = 256
VENC = 4
COILS = 8
ROWS_DEV = 64
SLICES = 8
PHASES = 4
ROWS = 256
CAP = 32
N_PHASE = 4


def place_ends(array, own_key, smallest, high):
    longest = array.shape.index(max(array.shape))
    spots = []
    for shift in (0, 1):
        where = [jax.random.randint(jax.random.fold_in(own_key, axis), (), 0, length) for axis, length in enumerate(array.shape)]
        where[longest] = (where[longest] + shift) % array.shape[longest]
        spots.append(tuple(where))
    return array.at[spots[0]].set(smallest).at[spots[1]].set(high)


def level_of(key, dims, shards, least, top_value):
    gain = 1.0
    for axis_at, blocks in shards:
        heights = jax.random.uniform(jax.random.fold_in(jax.random.fold_in(key, 6), axis_at), (blocks,), jnp.float32, least / len(shards), top_value / len(shards))
        gain = gain * jnp.repeat(jnp.exp(heights), dims[axis_at] // blocks).reshape((-1,) + (1,) * (len(dims) - 1 - axis_at))
    return gain


def assign_block(own_key, own, number, rows, amount, top, bound, lean):
    order = jax.random.permutation(own_key, amount)
    packed, common = load_shares(amount, rows * top, bound, lean, True), load_shares(amount, rows * top, bound, lean, False)
    places = jnp.arange(amount)

    def named(lengths, turn):
        used = int((lengths > 0).sum())
        fixed = max(1, used // 4)
        passed = fixed + (places - fixed + turn * (used - fixed)) % max(1, amount - fixed)
        return jnp.zeros((amount,), jnp.int32).at[order[jnp.where(places < fixed, places, passed)]].set(jnp.asarray(lengths, jnp.int32))

    lengths = jnp.where(number % 4 == 0, named(packed, number // 4), named(common, number - number // 4 - 1))
    mixed = jax.random.permutation(jax.random.fold_in(own, 3), amount)
    donor, taker = mixed[0:amount // 2 * 2:2], mixed[1:amount // 2 * 2:2]
    slack = jnp.minimum(lengths[donor] - 1, bound - lengths[taker]) // 2
    slack = jnp.where((donor == order[0]) | (taker == order[0]) | (lengths[taker] == 0), 0, jnp.maximum(slack, 0))
    passed = jax.random.randint(jax.random.fold_in(own, 4), (amount // 2,), 0, 1 << 20) % (slack + 1)
    lengths = lengths.at[donor].add(-passed).at[taker].add(passed)
    members = jnp.searchsorted(jnp.cumsum(lengths), jnp.arange(rows * top), side="right").astype(jnp.int32)
    listing = members.reshape(top, rows).T
    listing = listing[jax.random.permutation(jax.random.fold_in(own, 1), rows)]
    turn = jax.random.randint(jax.random.fold_in(own, 2), (rows, 1), 0, top)
    return jnp.take_along_axis(listing, (jnp.arange(top)[None, :] + turn) % top, axis=1)


def load_shares(number_of, total, most, skew, full):
    portions = [(1 << 20) // math.isqrt(grade ** skew) + 1 for grade in range(1, number_of + 1)]
    largest = most if full else min(most, max(-(-total // number_of), total * portions[0] // sum(portions)))
    least = 1 if total - largest >= number_of - 1 else 0
    holding, rest = [largest] + [least] * (number_of - 1), total - largest - least * (number_of - 1)
    while rest > 0:
        free = [i for i in range(1, number_of) if holding[i] < largest] or [i for i in range(1, number_of) if holding[i] < most]
        mass, remaining = sum([portions[i] for i in free]), rest
        for i in free:
            more = min(most - holding[i], max(1, remaining * portions[i] // mass), rest)
            holding[i] = holding[i] + more
            rest = rest - more
    return np.array(holding)


def gaussian(own_key, extent, deviation, bound, split=(), kind=jnp.bfloat16):
    level = level_of(own_key, extent, split, -0.22, 0.18) if split else 1.0
    drawn = jax.random.normal(own_key, extent, jnp.float32) * deviation * level
    return jnp.minimum(jnp.maximum(drawn, -bound), bound).astype(kind)


def setup_inputs(seed: int = 0) -> dict:
    arg_keys = jax.random.split(jax.random.key(seed), 6)
    image = gaussian(arg_keys[0], (PHASES, VENC, SLICES, NX, 2 * NY), 1.0, 6.0, ((0, 4), (2, 4)), jnp.float32)
    coil_maps = gaussian(arg_keys[1], (SLICES, COILS, NX, 2 * NY), 0.35, 2.0, ((0, 4), (1, 2)))
    kdata = gaussian(arg_keys[2], (ROWS, VENC, SLICES, COILS, 2 * NX), 1.0, 6.0, ((0, 4), (2, 4), (3, 2)))
    phase_bin_keys = jax.random.split(jax.random.fold_in(arg_keys[3], 1), ROWS // ROWS_DEV)
    phase_bin_turns = jax.random.permutation(jax.random.fold_in(arg_keys[3], 3), ROWS // ROWS_DEV)
    phase_bin = jax.vmap(lambda own, number: assign_block(jax.random.fold_in(arg_keys[3], 2), own, number, ROWS_DEV, PHASES, 1, CAP, 2))(phase_bin_keys, phase_bin_turns).reshape((ROWS, 1))
    line_index = place_ends(jax.random.randint(arg_keys[4], (ROWS,), 0, NY), jax.random.fold_in(arg_keys[4], 1), 0, NY - 1).astype(jnp.int32)
    return dict(image=image, coil_maps=coil_maps, kdata=kdata, phase_bin=phase_bin, line_index=line_index)


def reference(image, coil_maps, kdata, phase_bin, line_index):
    bins = phase_bin[:, 0]
    maps = coil_maps.astype(jnp.float32)
    sens = maps[..., :NY] + 1j * maps[..., NY:]
    limit = N_PHASE * CAP

    def one_phase(t):
        frame = image[t]
        field = frame[..., :NY] + 1j * frame[..., NY:]
        coil = field[:, :, None] * sens[None]
        kspace = jnp.fft.fft2(coil, norm="ortho")
        order = jnp.argsort((bins != t).astype(jnp.int32), stable=True)[:limit]
        chosen = line_index[order]
        valid = (bins[order] == t).astype(jnp.float32)
        pred = kspace[..., chosen]
        rows = kdata[order].astype(jnp.float32)
        measured = rows[..., :NX] + 1j * rows[..., NX:]
        measured = jnp.transpose(measured, (1, 2, 3, 4, 0))
        resid = (pred - measured) * valid
        grid = jnp.zeros_like(kspace).at[..., chosen].add(resid)
        back = jnp.fft.ifft2(grid, norm="ortho")
        combined = jnp.sum(jnp.conj(sens)[None] * back, axis=2)
        return jnp.concatenate([jnp.real(combined), jnp.imag(combined)], axis=-1).astype(jnp.float32)

    data_grad = lax.map(one_phase, jnp.arange(PHASES, dtype=jnp.int32))
    penalty = 2.0 * image - jnp.roll(image, 1, axis=0) - jnp.roll(image, -1, axis=0)
    return data_grad + 0.5 * penalty
```

```python
import functools
import math

import jax
import jax.numpy as jnp
import ml_dtypes
import numpy as np
from jax import lax
from jax.experimental import pallas as pl
from jax.experimental.pallas import tpu as pltpu
from jax.sharding import PartitionSpec as P


def passed_along(x, axis, by):
    devices = lax.axis_size(axis)
    return lax.ppermute(x, axis, [(i, (i + by) % devices) for i in range(devices)])


def split_numpy(table):
    high = table.astype(np.float32).astype(ml_dtypes.bfloat16)
    low = (table - high.astype(np.float64)).astype(np.float32).astype(ml_dtypes.bfloat16)
    return high, low


def inverse_table(count):
    steps = np.arange(count)
    angles = 2.0 * np.pi / count * (steps[:, None] * steps[None, :] % count)
    real_part = np.cos(angles) / math.sqrt(count)
    imag_part = np.sin(angles) / math.sqrt(count)
    return np.block([[real_part, -imag_part], [imag_part, real_part]])


def split(x):
    high = lax.reduce_precision(x, 8, 7)
    return high.astype(jnp.bfloat16), (x - high).astype(jnp.bfloat16)


def split_in_kernel(x):
    high = x.astype(jnp.bfloat16)
    return high, (x - high.astype(jnp.float32)).astype(jnp.bfloat16)


def expansion_table(lines, valid, count):
    steps = jnp.arange(count, dtype=jnp.int32)
    turns = lines[:, None] * steps[None, :] % count
    angles = 2.0 * math.pi / count * turns.astype(jnp.float32)
    factor = valid[:, None] / math.sqrt(count)
    real_part = jnp.cos(angles) * factor
    imag_part = jnp.sin(angles) * factor
    upper = jnp.concatenate([real_part, imag_part], axis=1)
    lower = jnp.concatenate([-imag_part, real_part], axis=1)
    return jnp.concatenate([upper, lower], axis=0)


def dot(a, b):
    return lax.dot_general(a, b, (((1,), (0,)), ((), ())), preferred_element_type=jnp.float32)


def dot_t(a, b):
    return lax.dot_general(a, b, (((1,), (1,)), ((), ())), preferred_element_type=jnp.float32)


def model_kernel(has_prior, _, image_ref, maps_ref, kh_ref, kl_ref, *rest):
    acc_ref, out_ref = rest if has_prior else (None, rest[0])
    own_venc, rows, twice_y = out_ref.shape[0], out_ref.shape[2], out_ref.shape[3]
    ncoil = maps_ref.shape[1]
    y = twice_y // 2
    for v in range(own_venc):
        x_re = image_ref[0, v, 0, :, :y]
        x_im = image_ref[0, v, 0, :, y:]
        parts = []
        for c in range(ncoil):
            s_re = maps_ref[0, c, :, :y].astype(jnp.float32)
            s_im = maps_ref[0, c, :, y:].astype(jnp.float32)
            parts.append(
                jnp.concatenate([s_re * x_re - s_im * x_im, s_re * x_im + s_im * x_re], axis=1)
            )
        high, low = split_in_kernel(jnp.concatenate(parts, axis=0))
        grid = dot(high, kh_ref[...]) + dot(low, kh_ref[...]) + dot(high, kl_ref[...])
        if has_prior:
            sum_re, sum_im = acc_ref[v, 0, :, :y], acc_ref[v, 0, :, y:]
        else:
            sum_re, sum_im = jnp.zeros_like(x_re), jnp.zeros_like(x_re)
        for c in range(ncoil):
            s_re = maps_ref[0, c, :, :y].astype(jnp.float32)
            s_im = maps_ref[0, c, :, y:].astype(jnp.float32)
            g_re = grid[c * rows:(c + 1) * rows, :y]
            g_im = grid[c * rows:(c + 1) * rows, y:]
            sum_re = sum_re + s_re * g_re + s_im * g_im
            sum_im = sum_im + s_re * g_im - s_im * g_re
        out_ref[v, 0, :, :y] = sum_re
        out_ref[v, 0, :, y:] = sum_im


def model_part(which, image, maps, kh, kl, acc, own_venc):
    _, _, slabs, width_x, twice_y = image.shape
    ncoil = maps.shape[1]
    block = 64
    in_specs = [
        pl.BlockSpec((1, own_venc, 1, block, twice_y), lambda s, i, w: (0, w[0], s, i, 0)),
        pl.BlockSpec((1, ncoil, block, twice_y), lambda s, i, w: (s, 0, i, 0)),
        pl.BlockSpec((twice_y, twice_y), lambda s, i, w: (0, 0)),
        pl.BlockSpec((twice_y, twice_y), lambda s, i, w: (0, 0)),
    ]
    out_spec = pl.BlockSpec((own_venc, 1, block, twice_y), lambda s, i, w: (0, s, i, 0))
    args = [which, image, maps, kh, kl]
    if acc is not None:
        in_specs.append(out_spec)
        args.append(acc)
    products = own_venc * slabs * ncoil * width_x
    return pl.pallas_call(
        functools.partial(model_kernel, acc is not None),
        out_shape=jax.ShapeDtypeStruct((own_venc, slabs, width_x, twice_y), jnp.float32),
        grid_spec=pltpu.PrefetchScalarGridSpec(
            num_scalar_prefetch=1, grid=(slabs, width_x // block), in_specs=in_specs, out_specs=out_spec
        ),
        compiler_params=pltpu.CompilerParams(vmem_limit_bytes=40 << 20),
        cost_estimate=pl.CostEstimate(
            flops=6 * products * twice_y * twice_y, bytes_accessed=8 << 20, transcendentals=0
        ),
        name="model_part",
    )(*args)


def data_kernel(final, _, rows_ref, maps_ref, th_ref, tl_ref, eh_ref, el_ref, acc_ref, *rest):
    if final:
        image_ref, prior_ref, later_ref, out_ref = rest
    else:
        (out_ref,) = rest
    slots = rows_ref.shape[0]
    ncoil, x, twice_y = maps_ref.shape[1], maps_ref.shape[2], maps_ref.shape[3]
    y = twice_y // 2
    twice_x = 2 * x
    sum_re = acc_ref[0, 0, :, :y]
    sum_im = acc_ref[0, 0, :, y:]
    for first in range(0, ncoil, 2):
        pair = jnp.concatenate(
            [rows_ref[:, c * twice_x:(c + 1) * twice_x] for c in (first, first + 1)], axis=0
        )
        along_x = dot_t(th_ref[...], pair) + dot_t(tl_ref[...], pair)
        lhs = jnp.concatenate(
            [
                jnp.concatenate(
                    [along_x[:x, i * slots:(i + 1) * slots], along_x[x:, i * slots:(i + 1) * slots]],
                    axis=1,
                )
                for i in (0, 1)
            ],
            axis=0,
        )
        high, low = split_in_kernel(lhs)
        grid = dot(high, eh_ref[...]) + dot(low, eh_ref[...]) + dot(high, el_ref[...])
        for i in (0, 1):
            s_re = maps_ref[0, first + i, :, :y].astype(jnp.float32)
            s_im = maps_ref[0, first + i, :, y:].astype(jnp.float32)
            g_re = grid[i * x:(i + 1) * x, :y]
            g_im = grid[i * x:(i + 1) * x, y:]
            sum_re = sum_re - (s_re * g_re + s_im * g_im)
            sum_im = sum_im - (s_re * g_im - s_im * g_re)
    if final:
        near = prior_ref[0, 0].astype(jnp.float32) + later_ref[0, 0].astype(jnp.float32)
        rest_term = image_ref[0, 0, 0] - 0.5 * near
        out_ref[0, 0, 0, :, :y] = sum_re + rest_term[:, :y]
        out_ref[0, 0, 0, :, y:] = sum_im + rest_term[:, y:]
    else:
        out_ref[0, 0, :, :y] = sum_re
        out_ref[0, 0, :, y:] = sum_im


def data_part(which, rows, maps, th, tl, eh, el, acc, own_venc, near=None):
    slots = rows.shape[0]
    slabs, ncoil, width_x, twice_y = maps.shape
    twice_x = 2 * width_x
    const = lambda s, v, w: (0, 0)
    frame = pl.BlockSpec((1, 1, width_x, twice_y), lambda s, v, w: (v, s, 0, 0))
    in_specs = [
        pl.BlockSpec((slots, ncoil * twice_x), lambda s, v, w: (0, v * slabs + s)),
        pl.BlockSpec((1, ncoil, width_x, twice_y), lambda s, v, w: (s, 0, 0, 0)),
        pl.BlockSpec((twice_x, twice_x), const),
        pl.BlockSpec((twice_x, twice_x), const),
        pl.BlockSpec((2 * slots, twice_y), const),
        pl.BlockSpec((2 * slots, twice_y), const),
        frame,
    ]
    args = [which, rows, maps, th, tl, eh, el, acc]
    if near is None:
        out_shape = jax.ShapeDtypeStruct((own_venc, slabs, width_x, twice_y), jnp.float32)
        out_spec = frame
    else:
        image, prior, later = near
        in_specs += [
            pl.BlockSpec((1, 1, 1, width_x, twice_y), lambda s, v, w: (0, w[0] * own_venc + v, s, 0, 0)),
            frame,
            frame,
        ]
        args += [image, prior, later]
        out_shape = jax.ShapeDtypeStruct((1, own_venc, slabs, width_x, twice_y), jnp.float32)
        out_spec = pl.BlockSpec((1, 1, 1, width_x, twice_y), lambda s, v, w: (0, v, s, 0, 0))
    products = own_venc * slabs * ncoil
    return pl.pallas_call(
        functools.partial(data_kernel, near is not None),
        out_shape=out_shape,
        grid_spec=pltpu.PrefetchScalarGridSpec(
            num_scalar_prefetch=1, grid=(slabs, own_venc), in_specs=in_specs, out_specs=out_spec
        ),
        compiler_params=pltpu.CompilerParams(vmem_limit_bytes=40 << 20),
        cost_estimate=pl.CostEstimate(
            flops=products * (4 * slots * twice_x * twice_x + 12 * slots * width_x * twice_y),
            bytes_accessed=8 << 20,
            transcendentals=0,
        ),
        name="data_part",
    )(*args)


def per_device(image, coil_maps, kdata, phase_bin, line_index):
    owners = lax.axis_size("phase")
    groups = lax.axis_size("coil")
    group = lax.axis_index("coil")
    rows = kdata.shape[0]
    venc, slabs, ncoil, twice_x = (kdata.shape[1], kdata.shape[2], kdata.shape[3], kdata.shape[4])
    width_x = twice_x // 2
    width_y = image.shape[-1] // 2
    own_venc = venc // groups
    feats = own_venc * slabs * ncoil * twice_x
    capacity = 2 * rows // owners
    slots = owners * capacity
    which = group.reshape(1).astype(jnp.int32)

    mine = lax.dynamic_slice_in_dim(image, group * own_venc, own_venc, 1)[0].astype(jnp.bfloat16)
    prior = passed_along(mine, "phase", 1)
    later = passed_along(mine, "phase", -1)

    all_rows, all_maps = [], []
    for k in range(groups):
        target = (group + k) % groups
        part = lax.dynamic_slice_in_dim(kdata, target * own_venc, own_venc, 1).reshape(rows, feats)
        all_rows.append(part if k == 0 else passed_along(part, "coil", k))
    for k in range(groups):
        all_maps.append(coil_maps if k == 0 else passed_along(coil_maps, "coil", k))

    bins = phase_bin[:, 0]
    hits = (bins[:, None] == jnp.arange(owners, dtype=jnp.int32)[None, :]).astype(jnp.int32)
    before = jnp.cumsum(hits, axis=0) - hits
    target = bins * capacity + jnp.sum(before * hits, axis=1)
    placing = target[None, :] == jnp.arange(slots, dtype=jnp.int32)[:, None]
    placing_int = placing.astype(jnp.int32)
    packed_lines = jnp.sum(placing_int * (line_index[None, :] + 1), axis=1) - 1
    lines_all = lax.all_to_all(
        packed_lines.reshape(owners, capacity), "phase", split_axis=0, concat_axis=0, tiled=True
    ).reshape(slots)
    valid = (lines_all >= 0).astype(jnp.float32)
    placing = placing.astype(jnp.bfloat16)

    arrived = []
    for k in range(groups):
        packed = jnp.dot(placing, all_rows[k], preferred_element_type=jnp.float32).astype(jnp.bfloat16)
        arrived.append(lax.all_to_all(packed, "phase", split_axis=0, concat_axis=0, tiled=True))

    etable = expansion_table(jnp.maximum(lines_all, 0), valid, width_y)
    eh, el = split(etable)
    ktable = jnp.dot(etable.T, etable, precision=lax.Precision.HIGHEST)
    kh, kl = split(ktable)
    th, tl = [jnp.asarray(t) for t in split_numpy(inverse_table(width_x))]

    acc = None
    for k in range(groups):
        acc = model_part(which, image, all_maps[k], kh, kl, acc, own_venc)
    for k in range(groups):
        near = (image, prior, later) if k == groups - 1 else None
        acc = data_part(which, arrived[k], all_maps[k], th, tl, eh, el, acc, own_venc, near)
    return acc


def solution(mesh):
    in_specs = (
        P("phase", None, "slab", None, None),
        P("slab", "coil", None, None),
        P("phase", None, "slab", "coil", None),
        P("phase", None),
        P("phase"),
    )
    out_specs = P("phase", "coil", "slab", None, None)
    return jax.shard_map(
        per_device, mesh=mesh, in_specs=in_specs, out_specs=out_specs, check_vma=False
    )
```

```python
import functools
import math

import jax
import jax.numpy as jnp
import ml_dtypes
import numpy as np
from jax import lax
from jax.experimental import pallas as pl
from jax.experimental.pallas import tpu as pltpu
from jax.sharding import PartitionSpec as P


MODEL_VMEM, DATA_VMEM, PACK_VMEM = 20 << 20, 24 << 20, 16 << 20


def passed_along(x, axis, by):
    devices = lax.axis_size(axis)
    return lax.ppermute(x, axis, [(i, (i + by) % devices) for i in range(devices)])


def split_numpy(table):
    high = table.astype(np.float32).astype(ml_dtypes.bfloat16)
    low = (table - high.astype(np.float64)).astype(np.float32).astype(ml_dtypes.bfloat16)
    return high, low


def inverse_table(count):
    steps = np.arange(count)
    angles = 2.0 * np.pi / count * (steps[:, None] * steps[None, :] % count)
    real_part = np.cos(angles) / math.sqrt(count)
    imag_part = np.sin(angles) / math.sqrt(count)
    return np.block([[real_part, -imag_part], [imag_part, real_part]])


def split(x):
    high = lax.reduce_precision(x, 8, 7)
    return high.astype(jnp.bfloat16), (x - high).astype(jnp.bfloat16)


def split_in_kernel(x):
    high = x.astype(jnp.bfloat16)
    return high, (x - high.astype(jnp.float32)).astype(jnp.bfloat16)


def expansion_table(lines, valid, count):
    steps = jnp.arange(count, dtype=jnp.int32)
    turns = lines[:, None] * steps[None, :] % count
    angles = 2.0 * math.pi / count * turns.astype(jnp.float32)
    factor = valid[:, None] / math.sqrt(count)
    real_part = jnp.cos(angles) * factor
    imag_part = jnp.sin(angles) * factor
    upper = jnp.concatenate([real_part, imag_part], axis=1)
    lower = jnp.concatenate([-imag_part, real_part], axis=1)
    return jnp.concatenate([upper, lower], axis=0)


def dot(a, b):
    return lax.dot_general(a, b, (((1,), (0,)), ((), ())), preferred_element_type=jnp.float32)


def dot_t(a, b):
    return lax.dot_general(a, b, (((1,), (1,)), ((), ())), preferred_element_type=jnp.float32)


def model_kernel(first, _, image_ref, maps_ref, k_ref, *rest):
    if first:
        prior_ref, later_ref, out_ref = rest
    else:
        acc_ref, out_ref = rest
    own_venc, rows, twice_y = out_ref.shape[0], out_ref.shape[2], out_ref.shape[3]
    ncoil = maps_ref.shape[1]
    y = twice_y // 2
    for v in range(own_venc):
        x_re = image_ref[0, v, 0, :, :y]
        x_im = image_ref[0, v, 0, :, y:]
        parts = []
        for c in range(ncoil):
            s_re = maps_ref[0, c, :, :y].astype(jnp.float32)
            s_im = maps_ref[0, c, :, y:].astype(jnp.float32)
            parts.append(
                jnp.concatenate([s_re * x_re - s_im * x_im, s_re * x_im + s_im * x_re], axis=1)
            )
        high, low = split_in_kernel(jnp.concatenate(parts, axis=0))
        grid = dot(high, k_ref[0]) + dot(low, k_ref[0]) + dot(high, k_ref[1])
        if first:
            near = prior_ref[v, 0].astype(jnp.float32) + later_ref[v, 0].astype(jnp.float32)
            sum_re = x_re - 0.5 * near[:, :y]
            sum_im = x_im - 0.5 * near[:, y:]
        else:
            sum_re, sum_im = acc_ref[v, 0, :, :y], acc_ref[v, 0, :, y:]
        for c in range(ncoil):
            s_re = maps_ref[0, c, :, :y].astype(jnp.float32)
            s_im = maps_ref[0, c, :, y:].astype(jnp.float32)
            g_re = grid[c * rows:(c + 1) * rows, :y]
            g_im = grid[c * rows:(c + 1) * rows, y:]
            sum_re = sum_re + s_re * g_re + s_im * g_im
            sum_im = sum_im + s_re * g_im - s_im * g_re
        out_ref[v, 0, :, :y] = sum_re
        out_ref[v, 0, :, y:] = sum_im


def model_part(which, image, maps, ktable, before, own_venc):
    _, _, slabs, width_x, twice_y = image.shape
    ncoil = maps.shape[1]
    block = 64
    out_spec = pl.BlockSpec((own_venc, 1, block, twice_y), lambda s, i, w: (0, s, i, 0))
    in_specs = [
        pl.BlockSpec((1, own_venc, 1, block, twice_y), lambda s, i, w: (0, w[0], s, i, 0)),
        pl.BlockSpec((1, ncoil, block, twice_y), lambda s, i, w: (s, 0, i, 0)),
        pl.BlockSpec((2, twice_y, twice_y), lambda s, i, w: (0, 0, 0)),
    ] + [out_spec] * len(before)
    products = own_venc * slabs * ncoil * width_x
    return pl.pallas_call(
        functools.partial(model_kernel, len(before) == 2),
        out_shape=jax.ShapeDtypeStruct((own_venc, slabs, width_x, twice_y), jnp.float32),
        grid_spec=pltpu.PrefetchScalarGridSpec(
            num_scalar_prefetch=1, grid=(slabs, width_x // block), in_specs=in_specs, out_specs=out_spec
        ),
        compiler_params=pltpu.CompilerParams(vmem_limit_bytes=MODEL_VMEM),
        cost_estimate=pl.CostEstimate(
            flops=6 * products * twice_y * twice_y, bytes_accessed=8 << 20, transcendentals=0
        ),
        name="model_part",
    )(which, image, maps, ktable, *before)


def pack_kernel(owners, capacity, at_ref, rows_ref, key_ref, *rest):
    outs, place_ref = rest[:-1], rest[-1]
    ncoil, twice_x = rows_ref.shape[3], rows_ref.shape[4]
    wide = key_ref.shape[1]
    total = owners * capacity

    @pl.when((pl.program_id(0) == 0) & (pl.program_id(1) == 0))
    def _():
        key = key_ref[...] - at_ref[1]
        key = jnp.where(key < 0, key + owners, key)
        owner = lax.broadcasted_iota(jnp.int32, (-(-owners // 8) * 8, wide), 0)
        hits = owner == key
        i = lax.broadcasted_iota(jnp.int32, (wide, wide), 0)
        j = lax.broadcasted_iota(jnp.int32, (wide, wide), 1)
        earlier = ((i // ncoil < j // ncoil) & (i % ncoil == 0)).astype(jnp.bfloat16)
        before = dot(hits.astype(jnp.bfloat16), earlier)
        rank = jnp.sum(jnp.where(hits, before, 0.0), axis=0, keepdims=True).astype(jnp.int32)
        target = key * capacity + rank
        a = lax.broadcasted_iota(jnp.int32, (ncoil * total, wide), 0)
        b = lax.broadcasted_iota(jnp.int32, (ncoil * total, wide), 1)
        place_ref[...] = ((a % total == target) & (a // total == b % ncoil)).astype(jnp.bfloat16)

    packed = dot(place_ref[...], rows_ref[:, 0, 0].reshape(wide, twice_x)).astype(jnp.bfloat16)
    height = total // len(outs)
    for c in range(ncoil):
        for k, out_ref in enumerate(outs):
            first = c * total + k * height
            out_ref[:, c * twice_x:(c + 1) * twice_x] = packed[first:first + height]


def pack(at, rows, key, owners, capacity, own_venc, pieces):
    count, _, slabs, ncoil, twice_x = rows.shape
    height = owners * capacity // pieces
    out_spec = pl.BlockSpec((height, ncoil * twice_x), lambda v, s, w: (0, v * slabs + s))
    out = jax.ShapeDtypeStruct((height, own_venc * slabs * ncoil * twice_x), jnp.bfloat16)
    return pl.pallas_call(
        functools.partial(pack_kernel, owners, capacity),
        out_shape=[out] * pieces,
        grid_spec=pltpu.PrefetchScalarGridSpec(
            num_scalar_prefetch=1,
            grid=(own_venc, slabs),
            in_specs=[
                pl.BlockSpec(
                    (count, 1, 1, ncoil, twice_x), lambda v, s, w: (0, w[0] * own_venc + v, s, 0, 0)
                ),
                pl.BlockSpec((1, count * ncoil), lambda v, s, w: (0, 0)),
            ],
            out_specs=[out_spec] * pieces,
            scratch_shapes=[pltpu.VMEM((ncoil * owners * capacity, count * ncoil), jnp.bfloat16)],
        ),
        compiler_params=pltpu.CompilerParams(vmem_limit_bytes=PACK_VMEM),
        name="pack",
    )(at, rows, key)


def data_kernel(count, *refs):
    rows_refs, (maps_ref, t_ref, e_ref, acc_ref, out_ref) = refs[:count], refs[count:]
    slots = e_ref.shape[0] // 6
    ncoil, x, twice_y = maps_ref.shape[1], maps_ref.shape[2], maps_ref.shape[3]
    y = twice_y // 2
    twice_x = 2 * x
    sum_re = acc_ref[0, 0, :, :y]
    sum_im = acc_ref[0, 0, :, y:]
    for first in range(0, ncoil, 4):
        pair = jnp.concatenate(
            [
                ref[:, c * twice_x:(c + 1) * twice_x]
                for c in range(first, first + 4)
                for ref in rows_refs
            ],
            axis=0,
        )
        along_x = dot_t(t_ref[...], jnp.concatenate([pair, pair], axis=1))
        lhs = jnp.concatenate(
            [
                jnp.concatenate(
                    [along_x[:x, i * slots:(i + 1) * slots], along_x[x:, i * slots:(i + 1) * slots]],
                    axis=1,
                )
                for i in range(4)
            ],
            axis=0,
        )
        high, low = split_in_kernel(lhs)
        grid = dot(jnp.concatenate([high, low, high], axis=1), e_ref[...])
        for i in range(4):
            s_re = maps_ref[0, first + i, :, :y].astype(jnp.float32)
            s_im = maps_ref[0, first + i, :, y:].astype(jnp.float32)
            g_re = grid[i * x:(i + 1) * x, :y]
            g_im = grid[i * x:(i + 1) * x, y:]
            sum_re = sum_re - (s_re * g_re + s_im * g_im)
            sum_im = sum_im - (s_re * g_im - s_im * g_re)
    out_ref[0, 0, :, :y] = sum_re
    out_ref[0, 0, :, y:] = sum_im


def data_part(rows, maps, ttable, etable, acc):
    capacity = rows[0].shape[0]
    slots = capacity * len(rows)
    own_venc = acc.shape[0]
    slabs, ncoil, width_x, twice_y = maps.shape
    twice_x = 2 * width_x
    const = lambda s, v: (0, 0)
    frame = pl.BlockSpec((1, 1, width_x, twice_y), lambda s, v: (v, s, 0, 0))
    products = own_venc * slabs * ncoil
    return pl.pallas_call(
        functools.partial(data_kernel, len(rows)),
        out_shape=jax.ShapeDtypeStruct(acc.shape, jnp.float32),
        grid=(slabs, own_venc),
        in_specs=[
            pl.BlockSpec((capacity, ncoil * twice_x), lambda s, v: (0, v * slabs + s)) for _ in rows
        ]
        + [
            pl.BlockSpec((1, ncoil, width_x, twice_y), lambda s, v: (s, 0, 0, 0)),
            pl.BlockSpec((twice_x, 2 * twice_x), const),
            pl.BlockSpec((6 * slots, twice_y), const),
            frame,
        ],
        out_specs=frame,
        compiler_params=pltpu.CompilerParams(vmem_limit_bytes=DATA_VMEM),
        cost_estimate=pl.CostEstimate(
            flops=products * (4 * slots * twice_x * twice_x + 12 * slots * width_x * twice_y),
            bytes_accessed=8 << 20,
            transcendentals=0,
        ),
        name="data_part",
    )(*rows, maps, ttable, etable, acc)


def per_device(image, coil_maps, kdata, phase_bin, line_index):
    owners = lax.axis_size("phase")
    groups = lax.axis_size("coil")
    group = lax.axis_index("coil")
    me = lax.axis_index("phase").astype(jnp.int32)
    rows = kdata.shape[0]
    venc, ncoil, twice_x = kdata.shape[1], kdata.shape[3], kdata.shape[4]
    width_x = twice_x // 2
    width_y = image.shape[-1] // 2
    own_venc = venc // groups
    capacity = 2 * rows // owners
    slots = owners * capacity
    which = group.reshape(1).astype(jnp.int32)
    zero = jnp.zeros((), jnp.int32)

    mine = lax.dynamic_slice_in_dim(image, group * own_venc, own_venc, 1)[0].astype(jnp.bfloat16)
    prior = passed_along(mine, "phase", 1)
    later = passed_along(mine, "phase", -1)

    others = []
    for k in range(1, groups):
        part = lax.dynamic_slice_in_dim(kdata, (group + k) % groups * own_venc, own_venc, 1)
        others.append(passed_along(part, "coil", k))
    late_maps, *others = lax.optimization_barrier((coil_maps, *others))
    all_maps = [coil_maps] + [passed_along(late_maps, "coil", k) for k in range(1, groups)]

    bins = phase_bin[:, 0]
    key = jnp.broadcast_to(bins[:, None], (rows, ncoil)).reshape(1, rows * ncoil)
    (packed,) = pack(jnp.stack([which[0], zero]), kdata, key, owners, capacity, own_venc, 1)
    arrived = [[lax.all_to_all(packed, "phase", split_axis=0, concat_axis=0, tiled=True)]]

    code, _ = lax.optimization_barrier((bins * width_y + line_index, mine))
    codes = jnp.stack([code] + [passed_along(code, "phase", k) for k in range(1, owners)])
    hits = codes // width_y == me
    rank = jnp.cumsum(hits.astype(jnp.int32), axis=1) - 1
    chosen = (rank[:, None] == jnp.arange(capacity, dtype=jnp.int32)[:, None]) & hits[:, None]
    lines = jnp.sum(jnp.where(chosen, (codes % width_y + 1)[:, None], 0), axis=2) - 1

    for other in others:
        pieces = pack(jnp.stack([zero, me]), other, key, owners, capacity, own_venc, owners)
        arrived.append([p if k == 0 else passed_along(p, "phase", k) for k, p in enumerate(pieces)])

    def tables(lines):
        lines = lines.reshape(slots)
        etable = expansion_table(jnp.maximum(lines, 0), (lines >= 0).astype(jnp.float32), width_y)
        high, low = split(etable)
        return etable, jnp.concatenate([high, high, low], axis=0)

    places = (me - jnp.arange(owners, dtype=jnp.int32)) % owners
    picked = (places[:, None] == jnp.arange(owners, dtype=jnp.int32)[None, :]).astype(jnp.int32)
    etable, e_other = tables(lines)
    _, e_first = tables(jnp.sum(picked[:, :, None] * lines[None], axis=1))
    ktable = jnp.dot(etable.T, etable, precision=lax.Precision.HIGHEST)
    ktable = jnp.stack(split(ktable))
    ttable = jnp.asarray(np.concatenate(split_numpy(inverse_table(width_x)), axis=1))

    acc = model_part(which, image, all_maps[0], ktable, (prior, later), own_venc)
    for k in range(1, groups):
        acc = model_part(which, image, all_maps[k], ktable, (acc,), own_venc)
    for k in range(groups):
        acc = data_part(arrived[k], all_maps[k], ttable, e_first if k == 0 else e_other, acc)
    return acc[None]


def solution(mesh):
    in_specs = (
        P("phase", None, "slab", None, None),
        P("slab", "coil", None, None),
        P("phase", None, "slab", "coil", None),
        P("phase", None),
        P("phase"),
    )
    out_specs = P("phase", "coil", "slab", None, None)
    return jax.shard_map(
        per_device, mesh=mesh, in_specs=in_specs, out_specs=out_specs, check_vma=False
    )
```

```python
import functools
import math

import jax
import jax.numpy as jnp
import ml_dtypes
import numpy as np
from jax import lax
from jax.experimental import pallas as pl
from jax.experimental.pallas import tpu as pltpu
from jax.sharding import PartitionSpec as P


MODEL_VMEM, DATA_VMEM, PACK_VMEM, OWN_VMEM = 20 << 20, 24 << 20, 16 << 20, 60 << 20


def passed_along(x, axis, by):
    devices = lax.axis_size(axis)
    return lax.ppermute(x, axis, [(i, (i + by) % devices) for i in range(devices)])


def split_numpy(table):
    high = table.astype(np.float32).astype(ml_dtypes.bfloat16)
    low = (table - high.astype(np.float64)).astype(np.float32).astype(ml_dtypes.bfloat16)
    return high, low


def inverse_table(count):
    steps = np.arange(count)
    angles = 2.0 * np.pi / count * (steps[:, None] * steps[None, :] % count)
    real_part = np.cos(angles) / math.sqrt(count)
    imag_part = np.sin(angles) / math.sqrt(count)
    return np.block([[real_part, -imag_part], [imag_part, real_part]])


def split(x):
    high = lax.reduce_precision(x, 8, 7)
    return high.astype(jnp.bfloat16), (x - high).astype(jnp.bfloat16)


def split_in_kernel(x):
    high = x.astype(jnp.bfloat16)
    return high, (x - high.astype(jnp.float32)).astype(jnp.bfloat16)


def expansion_table(lines, valid, count):
    steps = jnp.arange(count, dtype=jnp.int32)
    turns = lines[:, None] * steps[None, :] % count
    angles = 2.0 * math.pi / count * turns.astype(jnp.float32)
    factor = valid[:, None] / math.sqrt(count)
    real_part = jnp.cos(angles) * factor
    imag_part = jnp.sin(angles) * factor
    upper = jnp.concatenate([real_part, imag_part], axis=1)
    lower = jnp.concatenate([-imag_part, real_part], axis=1)
    return jnp.concatenate([upper, lower], axis=0)


def dot(a, b):
    return lax.dot_general(a, b, (((1,), (0,)), ((), ())), preferred_element_type=jnp.float32)


def dot_t(a, b):
    return lax.dot_general(a, b, (((1,), (1,)), ((), ())), preferred_element_type=jnp.float32)


def model_kernel(first, _, image_ref, maps_ref, k_ref, *rest):
    if first:
        prior_ref, later_ref, out_ref = rest
    else:
        acc_ref, out_ref = rest
    own_venc, rows, twice_y = out_ref.shape[0], out_ref.shape[2], out_ref.shape[3]
    ncoil = maps_ref.shape[1]
    y = twice_y // 2
    for v in range(own_venc):
        x_re = image_ref[0, v, 0, :, :y]
        x_im = image_ref[0, v, 0, :, y:]
        parts = []
        for c in range(ncoil):
            s_re = maps_ref[0, c, :, :y].astype(jnp.float32)
            s_im = maps_ref[0, c, :, y:].astype(jnp.float32)
            parts.append(
                jnp.concatenate([s_re * x_re - s_im * x_im, s_re * x_im + s_im * x_re], axis=1)
            )
        high, low = split_in_kernel(jnp.concatenate(parts, axis=0))
        grid = dot(high, k_ref[0]) + dot(low, k_ref[0]) + dot(high, k_ref[1])
        if first:
            near = prior_ref[v, 0].astype(jnp.float32) + later_ref[v, 0].astype(jnp.float32)
            sum_re = x_re - 0.5 * near[:, :y]
            sum_im = x_im - 0.5 * near[:, y:]
        else:
            sum_re, sum_im = acc_ref[v, 0, :, :y], acc_ref[v, 0, :, y:]
        for c in range(ncoil):
            s_re = maps_ref[0, c, :, :y].astype(jnp.float32)
            s_im = maps_ref[0, c, :, y:].astype(jnp.float32)
            g_re = grid[c * rows:(c + 1) * rows, :y]
            g_im = grid[c * rows:(c + 1) * rows, y:]
            sum_re = sum_re + s_re * g_re + s_im * g_im
            sum_im = sum_im + s_re * g_im - s_im * g_re
        out_ref[v, 0, :, :y] = sum_re
        out_ref[v, 0, :, y:] = sum_im


def model_part(which, image, maps, ktable, before, own_venc):
    _, _, slabs, width_x, twice_y = image.shape
    ncoil = maps.shape[1]
    block = 64
    out_spec = pl.BlockSpec((own_venc, 1, block, twice_y), lambda s, i, w: (0, s, i, 0))
    in_specs = [
        pl.BlockSpec((1, own_venc, 1, block, twice_y), lambda s, i, w: (0, w[0], s, i, 0)),
        pl.BlockSpec((1, ncoil, block, twice_y), lambda s, i, w: (s, 0, i, 0)),
        pl.BlockSpec((2, twice_y, twice_y), lambda s, i, w: (0, 0, 0)),
    ] + [out_spec] * len(before)
    products = own_venc * slabs * ncoil * width_x
    return pl.pallas_call(
        functools.partial(model_kernel, len(before) == 2),
        out_shape=jax.ShapeDtypeStruct((own_venc, slabs, width_x, twice_y), jnp.float32),
        grid_spec=pltpu.PrefetchScalarGridSpec(
            num_scalar_prefetch=1, grid=(slabs, width_x // block), in_specs=in_specs, out_specs=out_spec
        ),
        compiler_params=pltpu.CompilerParams(vmem_limit_bytes=MODEL_VMEM),
        cost_estimate=pl.CostEstimate(
            flops=6 * products * twice_y * twice_y, bytes_accessed=8 << 20, transcendentals=0
        ),
        name="model_part",
    )(which, image, maps, ktable, *before)


def pack_kernel(owners, capacity, pieces, at_ref, rows_ref, key_ref, *rest):
    outs, place_ref = rest[:-1], rest[-1]
    ncoil, twice_x = rows_ref.shape[3], rows_ref.shape[4]
    wide = key_ref.shape[1]
    total = owners * capacity

    @pl.when(pl.program_id(0) == 0)
    def _():
        key = key_ref[...] - at_ref[1]
        key = jnp.where(key < 0, key + owners, key)
        owner = lax.broadcasted_iota(jnp.int32, (-(-owners // 8) * 8, wide), 0)
        hits = owner == key
        i = lax.broadcasted_iota(jnp.int32, (wide, wide), 0)
        j = lax.broadcasted_iota(jnp.int32, (wide, wide), 1)
        earlier = ((i // ncoil < j // ncoil) & (i % ncoil == 0)).astype(jnp.bfloat16)
        before = dot(hits.astype(jnp.bfloat16), earlier)
        rank = jnp.sum(jnp.where(hits, before, 0.0), axis=0, keepdims=True).astype(jnp.int32)
        target = key * capacity + rank
        a = lax.broadcasted_iota(jnp.int32, (ncoil * total, wide), 0)
        b = lax.broadcasted_iota(jnp.int32, (ncoil * total, wide), 1)
        place_ref[...] = ((a % total == target) & (a // total == b % ncoil)).astype(jnp.bfloat16)

    own_venc = rows_ref.shape[1]
    for v in range(own_venc):
        packed = dot(place_ref[...], rows_ref[:, v, 0].reshape(wide, twice_x)).astype(jnp.bfloat16)
        for (first, height, only), out_ref in zip(pieces, outs):
            if only is None or only == v:
                for c in range(ncoil):
                    lane = (c if only == v else v * ncoil + c) * twice_x
                    start = c * total + first
                    out_ref[:, lane:lane + twice_x] = packed[start:start + height]


def pack(at, rows, key, owners, capacity, own_venc, pieces):
    count, _, slabs, ncoil, twice_x = rows.shape
    shapes = [(h, ncoil * twice_x * (own_venc if v is None else 1)) for _, h, v in pieces]
    return pl.pallas_call(
        functools.partial(pack_kernel, owners, capacity, pieces),
        out_shape=[jax.ShapeDtypeStruct((h, slabs * w), jnp.bfloat16) for h, w in shapes],
        grid_spec=pltpu.PrefetchScalarGridSpec(
            num_scalar_prefetch=1,
            grid=(slabs,),
            in_specs=[
                pl.BlockSpec((count, own_venc, 1, ncoil, twice_x), lambda s, w: (0, w[0], s, 0, 0)),
                pl.BlockSpec((1, count * ncoil), lambda s, w: (0, 0)),
            ],
            out_specs=[pl.BlockSpec(shape, lambda s, w: (0, s)) for shape in shapes],
            scratch_shapes=[pltpu.VMEM((ncoil * owners * capacity, count * ncoil), jnp.bfloat16)],
        ),
        compiler_params=pltpu.CompilerParams(vmem_limit_bytes=PACK_VMEM),
        name="pack",
    )(at, rows, key)


def data_kernel(count, *refs):
    rows_refs, (maps_ref, t_ref, e_ref, acc_ref, out_ref) = refs[:count], refs[count:]
    slots = e_ref.shape[0] // 6
    ncoil, x, twice_y = maps_ref.shape[1], maps_ref.shape[2], maps_ref.shape[3]
    y = twice_y // 2
    twice_x = 2 * x
    sum_re = acc_ref[0, 0, :, :y]
    sum_im = acc_ref[0, 0, :, y:]
    for first in range(0, ncoil, 4):
        pair = jnp.concatenate(
            [
                ref[:, c * twice_x:(c + 1) * twice_x]
                for c in range(first, first + 4)
                for ref in rows_refs
            ],
            axis=0,
        )
        along_x = dot_t(t_ref[...], jnp.concatenate([pair, pair], axis=1))
        lhs = jnp.concatenate(
            [
                jnp.concatenate(
                    [along_x[:x, i * slots:(i + 1) * slots], along_x[x:, i * slots:(i + 1) * slots]],
                    axis=1,
                )
                for i in range(4)
            ],
            axis=0,
        )
        high, low = split_in_kernel(lhs)
        grid = dot(jnp.concatenate([high, low, high], axis=1), e_ref[...])
        for i in range(4):
            s_re = maps_ref[0, first + i, :, :y].astype(jnp.float32)
            s_im = maps_ref[0, first + i, :, y:].astype(jnp.float32)
            g_re = grid[i * x:(i + 1) * x, :y]
            g_im = grid[i * x:(i + 1) * x, y:]
            sum_re = sum_re - (s_re * g_re + s_im * g_im)
            sum_im = sum_im - (s_re * g_im - s_im * g_re)
    out_ref[0, 0, :, :y] = sum_re
    out_ref[0, 0, :, y:] = sum_im


def data_part(rows, maps, ttable, etable, acc, encodings):
    capacity = rows[0][0].shape[0]
    slots = capacity * len(rows)
    own_venc = acc.shape[0]
    slabs, ncoil, width_x, twice_y = maps.shape
    twice_x = 2 * width_x
    first, count = encodings
    const = lambda s, v: (0, 0)
    frame = pl.BlockSpec((1, 1, width_x, twice_y), lambda s, v: (first + v, s, 0, 0))
    products = count * slabs * ncoil
    return pl.pallas_call(
        functools.partial(data_kernel, len(rows)),
        out_shape=jax.ShapeDtypeStruct(acc.shape, jnp.float32),
        grid=(slabs, count),
        in_specs=[
            pl.BlockSpec(
                (capacity, ncoil * twice_x), lambda s, v, every=every: (0, s * own_venc + first + v if every else s)
            )
            for _, every in rows
        ]
        + [
            pl.BlockSpec((1, ncoil, width_x, twice_y), lambda s, v: (s, 0, 0, 0)),
            pl.BlockSpec((twice_x, 2 * twice_x), const),
            pl.BlockSpec((6 * slots, twice_y), const),
            frame,
        ],
        out_specs=frame,
        input_output_aliases={len(rows) + 3: 0},
        compiler_params=pltpu.CompilerParams(vmem_limit_bytes=DATA_VMEM),
        cost_estimate=pl.CostEstimate(
            flops=products * (4 * slots * twice_x * twice_x + 12 * slots * width_x * twice_y),
            bytes_accessed=8 << 20,
            transcendentals=0,
        ),
        name="data_part",
    )(*[array for array, _ in rows], maps, ttable, etable, acc)


def own_image_kernel(which_ref, image_ref, out_ref, wide_ref, narrow_ref, in_sems, out_sems):
    own_venc, slabs = out_ref.shape[0], out_ref.shape[1]
    frames = [(v, s) for v in range(own_venc) for s in range(slabs)]
    first = which_ref[0] * own_venc
    fetches = [
        pltpu.make_async_copy(image_ref.at[0, first + v, s], wide_ref.at[i], in_sems.at[i])
        for i, (v, s) in enumerate(frames)
    ]
    for fetch in fetches:
        fetch.start()
    stores = [
        pltpu.make_async_copy(narrow_ref.at[i], out_ref.at[v, s], out_sems.at[i])
        for i, (v, s) in enumerate(frames)
    ]
    for i, (fetch, store) in enumerate(zip(fetches, stores)):
        fetch.wait()
        narrow_ref[i] = wide_ref[i].astype(jnp.bfloat16)
        store.start()
    for store in stores:
        store.wait()


def own_image(which, image, own_venc):
    _, _, slabs, width_x, twice_y = image.shape
    frames = (own_venc * slabs, width_x, twice_y)
    return pl.pallas_call(
        own_image_kernel,
        out_shape=jax.ShapeDtypeStruct((own_venc, slabs, width_x, twice_y), jnp.bfloat16),
        in_specs=[pl.BlockSpec(memory_space=pltpu.SMEM), pl.BlockSpec(memory_space=pl.ANY)],
        out_specs=pl.BlockSpec(memory_space=pl.ANY),
        scratch_shapes=[
            pltpu.VMEM(frames, jnp.float32),
            pltpu.VMEM(frames, jnp.bfloat16),
            pltpu.SemaphoreType.DMA(frames[:1]),
            pltpu.SemaphoreType.DMA(frames[:1]),
        ],
        compiler_params=pltpu.CompilerParams(vmem_limit_bytes=OWN_VMEM),
        name="own_image",
    )(which, image)


def per_device(image, coil_maps, kdata, phase_bin, line_index):
    owners = lax.axis_size("phase")
    groups = lax.axis_size("coil")
    group = lax.axis_index("coil")
    me = lax.axis_index("phase").astype(jnp.int32)
    rows = kdata.shape[0]
    venc, ncoil, twice_x = kdata.shape[1], kdata.shape[3], kdata.shape[4]
    width_x = twice_x // 2
    width_y = image.shape[-1] // 2
    own_venc = venc // groups
    capacity = 2 * rows // owners
    slots = owners * capacity
    which = group.reshape(1).astype(jnp.int32)
    zero = jnp.zeros((), jnp.int32)

    mine = own_image(which, image, own_venc)
    prior = passed_along(mine, "phase", 1)
    later = passed_along(mine, "phase", -1)

    others = []
    for k in range(1, groups):
        part = lax.dynamic_slice_in_dim(kdata, (group + k) % groups * own_venc, own_venc, 1)
        others.append(passed_along(part, "coil", k))
    late_maps, *others = lax.optimization_barrier((coil_maps, *others))
    all_maps = [coil_maps] + [passed_along(late_maps, "coil", k) for k in range(1, groups)]

    bins = phase_bin[:, 0]
    key = jnp.broadcast_to(bins[:, None], (rows, ncoil)).reshape(1, rows * ncoil)
    (packed,) = pack(jnp.stack([which[0], zero]), kdata, key, owners, capacity, own_venc, [(0, slots, None)])
    first = lax.all_to_all(packed, "phase", split_axis=0, concat_axis=0, tiled=True)

    code, _ = lax.optimization_barrier((bins * width_y + line_index, mine))
    codes = jnp.stack([code] + [passed_along(code, "phase", k) for k in range(1, owners)])
    hits = codes // width_y == me
    rank = jnp.cumsum(hits.astype(jnp.int32), axis=1) - 1
    chosen = (rank[:, None] == jnp.arange(capacity, dtype=jnp.int32)[:, None]) & hits[:, None]
    lines = jnp.sum(jnp.where(chosen, (codes % width_y + 1)[:, None], 0), axis=2) - 1

    arrived = []
    places = [(k, v) for k in (0, 1) for v in [None]] + [(k, v) for v in range(own_venc) for k in range(2, owners)]
    for other in others:
        pieces = [(k * capacity, capacity, v) for k, v in places]
        packed = pack(jnp.stack([zero, me]), other, key, owners, capacity, own_venc, pieces)
        moved = {
            place: (p if place[0] == 0 else passed_along(p, "phase", place[0]), place[1] is None)
            for place, p in zip(places, packed)
        }
        for v in range(own_venc):
            arrived.append([moved[k, None] for k in (0, 1)] + [moved[k, v] for k in range(2, owners)])

    def tables(lines):
        lines = lines.reshape(slots)
        etable = expansion_table(jnp.maximum(lines, 0), (lines >= 0).astype(jnp.float32), width_y)
        high, low = split(etable)
        return etable, jnp.concatenate([high, high, low], axis=0)

    places = (me - jnp.arange(owners, dtype=jnp.int32)) % owners
    picked = (places[:, None] == jnp.arange(owners, dtype=jnp.int32)[None, :]).astype(jnp.int32)
    etable, e_other = tables(lines)
    _, e_first = tables(jnp.sum(picked[:, :, None] * lines[None], axis=1))
    ktable = jnp.dot(etable.T, etable, precision=lax.Precision.HIGHEST)
    ktable = jnp.stack(split(ktable))
    ttable = jnp.asarray(np.concatenate(split_numpy(inverse_table(width_x)), axis=1))

    acc = model_part(which, image, all_maps[0], ktable, (prior, later), own_venc)
    for k in range(1, groups):
        acc = model_part(which, image, all_maps[k], ktable, (acc,), own_venc)
    acc = data_part([(first, True)], all_maps[0], ttable, e_first, acc, (0, own_venc))
    for k, blocks in enumerate(arrived):
        acc = data_part(blocks, all_maps[1 + k // own_venc], ttable, e_other, acc, (k % own_venc, 1))
    return acc[None]


def solution(mesh):
    in_specs = (
        P("phase", None, "slab", None, None),
        P("slab", "coil", None, None),
        P("phase", None, "slab", "coil", None),
        P("phase", None),
        P("phase"),
    )
    out_specs = P("phase", "coil", "slab", None, None)
    return jax.shard_map(
        per_device, mesh=mesh, in_specs=in_specs, out_specs=out_specs, check_vma=False
    )
```

```python
import functools
import math

import jax
import jax.numpy as jnp
import ml_dtypes
import numpy as np
from jax import lax
from jax.experimental import pallas as pl
from jax.experimental.pallas import tpu as pltpu
from jax.sharding import PartitionSpec as P


MODEL_VMEM, DATA_VMEM, PACK_VMEM, OWN_VMEM = 20 << 20, 24 << 20, 16 << 20, 60 << 20


def passed_along(x, axis, by):
    devices = lax.axis_size(axis)
    return lax.ppermute(x, axis, [(i, (i + by) % devices) for i in range(devices)])


def split_numpy(table):
    high = table.astype(np.float32).astype(ml_dtypes.bfloat16)
    low = (table - high.astype(np.float64)).astype(np.float32).astype(ml_dtypes.bfloat16)
    return high, low


def inverse_table(count):
    steps = np.arange(count)
    angles = 2.0 * np.pi / count * (steps[:, None] * steps[None, :] % count)
    real_part = np.cos(angles) / math.sqrt(count)
    imag_part = np.sin(angles) / math.sqrt(count)
    return np.block([[real_part, -imag_part], [imag_part, real_part]])


def split(x):
    high = lax.reduce_precision(x, 8, 7)
    return high.astype(jnp.bfloat16), (x - high).astype(jnp.bfloat16)


def split_in_kernel(x):
    high = x.astype(jnp.bfloat16)
    return high, (x - high.astype(jnp.float32)).astype(jnp.bfloat16)


def expansion_table(lines, valid, count):
    steps = jnp.arange(count, dtype=jnp.int32)
    turns = lines[:, None] * steps[None, :] % count
    angles = 2.0 * math.pi / count * turns.astype(jnp.float32)
    factor = valid[:, None] / math.sqrt(count)
    real_part = jnp.cos(angles) * factor
    imag_part = jnp.sin(angles) * factor
    upper = jnp.concatenate([real_part, imag_part], axis=1)
    lower = jnp.concatenate([-imag_part, real_part], axis=1)
    return jnp.concatenate([upper, lower], axis=0)


def dot(a, b):
    return lax.dot_general(a, b, (((1,), (0,)), ((), ())), preferred_element_type=jnp.float32)


def dot_t(a, b):
    return lax.dot_general(a, b, (((1,), (1,)), ((), ())), preferred_element_type=jnp.float32)


def model_kernel(first, _, image_ref, maps_ref, k_ref, *rest):
    if first:
        near_refs, out_ref = rest[:-1], rest[-1]
    else:
        acc_ref, out_ref = rest
    own_venc, rows, twice_y = out_ref.shape[0], out_ref.shape[2], out_ref.shape[3]
    ncoil = maps_ref.shape[1]
    y = twice_y // 2
    for v in range(own_venc):
        x_re = image_ref[0, v, 0, :, :y]
        x_im = image_ref[0, v, 0, :, y:]
        parts = []
        for c in range(ncoil):
            s_re = maps_ref[0, c, :, :y].astype(jnp.float32)
            s_im = maps_ref[0, c, :, y:].astype(jnp.float32)
            parts.append(
                jnp.concatenate([s_re * x_re - s_im * x_im, s_re * x_im + s_im * x_re], axis=1)
            )
        high, low = split_in_kernel(jnp.concatenate(parts, axis=0))
        grid = dot(high, k_ref[0]) + dot(low, k_ref[0]) + dot(high, k_ref[1])
        if first:
            near = near_refs[2 * v][...].astype(jnp.float32) + near_refs[2 * v + 1][...].astype(jnp.float32)
            sum_re = x_re - 0.5 * near[:, :y]
            sum_im = x_im - 0.5 * near[:, y:]
        else:
            sum_re, sum_im = acc_ref[v, 0, :, :y], acc_ref[v, 0, :, y:]
        for c in range(ncoil):
            s_re = maps_ref[0, c, :, :y].astype(jnp.float32)
            s_im = maps_ref[0, c, :, y:].astype(jnp.float32)
            g_re = grid[c * rows:(c + 1) * rows, :y]
            g_im = grid[c * rows:(c + 1) * rows, y:]
            sum_re = sum_re + s_re * g_re + s_im * g_im
            sum_im = sum_im + s_re * g_im - s_im * g_re
        out_ref[v, 0, :, :y] = sum_re
        out_ref[v, 0, :, y:] = sum_im


def model_part(which, image, maps, ktable, before, own_venc):
    _, _, slabs, width_x, twice_y = image.shape
    ncoil = maps.shape[1]
    block = 64
    out_spec = pl.BlockSpec((own_venc, 1, block, twice_y), lambda s, i, w: (0, s, i, 0))
    in_specs = [
        pl.BlockSpec((1, own_venc, 1, block, twice_y), lambda s, i, w: (0, w[0], s, i, 0)),
        pl.BlockSpec((1, ncoil, block, twice_y), lambda s, i, w: (s, 0, i, 0)),
        pl.BlockSpec((2, twice_y, twice_y), lambda s, i, w: (0, 0, 0)),
    ]
    if len(before) == 2:
        steps = width_x // block
        near_specs = [
            pl.BlockSpec((block, twice_y), lambda s, i, w, v=v: ((v * slabs + s) * steps + i, 0))
            for v in range(own_venc)
        ]
        in_specs += [spec for spec in near_specs for _ in before]
        args = list(before) * own_venc
    else:
        in_specs.append(out_spec)
        args = list(before)
    products = own_venc * slabs * ncoil * width_x
    return pl.pallas_call(
        functools.partial(model_kernel, len(before) == 2),
        out_shape=jax.ShapeDtypeStruct((own_venc, slabs, width_x, twice_y), jnp.float32),
        grid_spec=pltpu.PrefetchScalarGridSpec(
            num_scalar_prefetch=1, grid=(slabs, width_x // block), in_specs=in_specs, out_specs=out_spec
        ),
        compiler_params=pltpu.CompilerParams(vmem_limit_bytes=MODEL_VMEM),
        cost_estimate=pl.CostEstimate(
            flops=6 * products * twice_y * twice_y, bytes_accessed=8 << 20, transcendentals=0
        ),
        name="model_part",
    )(which, image, maps, ktable, *args)


def pack_kernel(owners, capacity, pieces, at_ref, rows_ref, key_ref, *rest):
    outs, place_ref = rest[:-1], rest[-1]
    ncoil, twice_x = rows_ref.shape[3], rows_ref.shape[4]
    wide = key_ref.shape[1]
    total = owners * capacity

    @pl.when(pl.program_id(0) == 0)
    def _():
        key = key_ref[...] - at_ref[1]
        key = jnp.where(key < 0, key + owners, key)
        owner = lax.broadcasted_iota(jnp.int32, (-(-owners // 8) * 8, wide), 0)
        hits = owner == key
        i = lax.broadcasted_iota(jnp.int32, (wide, wide), 0)
        j = lax.broadcasted_iota(jnp.int32, (wide, wide), 1)
        earlier = ((i // ncoil < j // ncoil) & (i % ncoil == 0)).astype(jnp.bfloat16)
        before = dot(hits.astype(jnp.bfloat16), earlier)
        rank = jnp.sum(jnp.where(hits, before, 0.0), axis=0, keepdims=True).astype(jnp.int32)
        target = key * capacity + rank
        a = lax.broadcasted_iota(jnp.int32, (ncoil * total, wide), 0)
        b = lax.broadcasted_iota(jnp.int32, (ncoil * total, wide), 1)
        place_ref[...] = ((a % total == target) & (a // total == b % ncoil)).astype(jnp.bfloat16)

    own_venc = rows_ref.shape[1]
    for v in range(own_venc):
        packed = dot(place_ref[...], rows_ref[:, v, 0].reshape(wide, twice_x)).astype(jnp.bfloat16)
        for (first, height, only), out_ref in zip(pieces, outs):
            if only is None or only == v:
                for c in range(ncoil):
                    lane = (c if only == v else v * ncoil + c) * twice_x
                    start = c * total + first
                    out_ref[:, lane:lane + twice_x] = packed[start:start + height]


def pack(at, rows, key, owners, capacity, own_venc, pieces):
    count, _, slabs, ncoil, twice_x = rows.shape
    shapes = [(h, ncoil * twice_x * (own_venc if v is None else 1)) for _, h, v in pieces]
    return pl.pallas_call(
        functools.partial(pack_kernel, owners, capacity, pieces),
        out_shape=[jax.ShapeDtypeStruct((h, slabs * w), jnp.bfloat16) for h, w in shapes],
        grid_spec=pltpu.PrefetchScalarGridSpec(
            num_scalar_prefetch=1,
            grid=(slabs,),
            in_specs=[
                pl.BlockSpec((count, own_venc, 1, ncoil, twice_x), lambda s, w: (0, w[0], s, 0, 0)),
                pl.BlockSpec((1, count * ncoil), lambda s, w: (0, 0)),
            ],
            out_specs=[pl.BlockSpec(shape, lambda s, w: (0, s)) for shape in shapes],
            scratch_shapes=[pltpu.VMEM((ncoil * owners * capacity, count * ncoil), jnp.bfloat16)],
        ),
        compiler_params=pltpu.CompilerParams(vmem_limit_bytes=PACK_VMEM),
        name="pack",
    )(at, rows, key)


def data_kernel(count, *refs):
    rows_refs, (maps_ref, t_ref, e_ref, acc_ref, out_ref) = refs[:count], refs[count:]
    slots = e_ref.shape[0] // 6
    ncoil, x, twice_y = maps_ref.shape[1], maps_ref.shape[2], maps_ref.shape[3]
    y = twice_y // 2
    twice_x = 2 * x
    sum_re = acc_ref[0, 0, :, :y]
    sum_im = acc_ref[0, 0, :, y:]
    for first in range(0, ncoil, 4):
        pair = jnp.concatenate(
            [
                ref[:, c * twice_x:(c + 1) * twice_x]
                for c in range(first, first + 4)
                for ref in rows_refs
            ],
            axis=0,
        )
        along_x = dot_t(t_ref[...], jnp.concatenate([pair, pair], axis=1))
        lhs = jnp.concatenate(
            [
                jnp.concatenate(
                    [along_x[:x, i * slots:(i + 1) * slots], along_x[x:, i * slots:(i + 1) * slots]],
                    axis=1,
                )
                for i in range(4)
            ],
            axis=0,
        )
        high, low = split_in_kernel(lhs)
        grid = dot(jnp.concatenate([high, low, high], axis=1), e_ref[...])
        for i in range(4):
            s_re = maps_ref[0, first + i, :, :y].astype(jnp.float32)
            s_im = maps_ref[0, first + i, :, y:].astype(jnp.float32)
            g_re = grid[i * x:(i + 1) * x, :y]
            g_im = grid[i * x:(i + 1) * x, y:]
            sum_re = sum_re - (s_re * g_re + s_im * g_im)
            sum_im = sum_im - (s_re * g_im - s_im * g_re)
    out_ref[0, 0, :, :y] = sum_re
    out_ref[0, 0, :, y:] = sum_im


def data_part(rows, maps, ttable, etable, acc, encodings):
    capacity = rows[0][0].shape[0]
    slots = capacity * len(rows)
    own_venc = acc.shape[0]
    slabs, ncoil, width_x, twice_y = maps.shape
    twice_x = 2 * width_x
    first, count = encodings
    const = lambda s, v: (0, 0)
    frame = pl.BlockSpec((1, 1, width_x, twice_y), lambda s, v: (first + v, s, 0, 0))
    products = count * slabs * ncoil
    return pl.pallas_call(
        functools.partial(data_kernel, len(rows)),
        out_shape=jax.ShapeDtypeStruct(acc.shape, jnp.float32),
        grid=(slabs, count),
        in_specs=[
            pl.BlockSpec(
                (capacity, ncoil * twice_x), lambda s, v, every=every: (0, s * own_venc + first + v if every else s)
            )
            for _, every in rows
        ]
        + [
            pl.BlockSpec((1, ncoil, width_x, twice_y), lambda s, v: (s, 0, 0, 0)),
            pl.BlockSpec((twice_x, 2 * twice_x), const),
            pl.BlockSpec((6 * slots, twice_y), const),
            frame,
        ],
        out_specs=frame,
        input_output_aliases={len(rows) + 3: 0},
        compiler_params=pltpu.CompilerParams(vmem_limit_bytes=DATA_VMEM),
        cost_estimate=pl.CostEstimate(
            flops=products * (4 * slots * twice_x * twice_x + 12 * slots * width_x * twice_y),
            bytes_accessed=8 << 20,
            transcendentals=0,
        ),
        name="data_part",
    )(*[array for array, _ in rows], maps, ttable, etable, acc)


def own_image_kernel(which_ref, image_ref, bins_ref, lines_ref, out_ref, wide_ref, narrow_ref, in_sems, out_sems):
    count, width_x = wide_ref.shape[0], wide_ref.shape[1]
    slabs = image_ref.shape[2]
    own_venc = count // slabs
    rows = bins_ref.shape[1]
    first = which_ref[0] * own_venc
    fetches = [
        pltpu.make_async_copy(image_ref.at[0, first + i // slabs, i % slabs], wide_ref.at[i], in_sems.at[i])
        for i in range(count)
    ]
    for fetch in fetches:
        fetch.start()
    spans = [pl.ds(i * width_x, width_x) for i in range(count)] + [pl.ds(count * width_x, 16)]
    stores = [
        pltpu.make_async_copy(narrow_ref.at[span], out_ref.at[span], out_sems.at[i])
        for i, span in enumerate(spans)
    ]
    narrow_ref[spans[-1], :] = jnp.zeros((16, narrow_ref.shape[1]), jnp.bfloat16)
    for lane, values in ((0, bins_ref), (128, lines_ref)):
        block = jnp.broadcast_to(values[...].astype(jnp.float32), (16, rows))
        narrow_ref[spans[-1], lane:lane + rows] = block.astype(jnp.bfloat16)
    stores[-1].start()
    for i, (fetch, store) in enumerate(zip(fetches, stores)):
        fetch.wait()
        narrow_ref[spans[i], :] = wide_ref[i].astype(jnp.bfloat16)
        store.start()
    for store in stores:
        store.wait()


def own_image(which, image, bins, lines, own_venc):
    _, _, slabs, width_x, twice_y = image.shape
    count = own_venc * slabs
    height = count * width_x + 16
    in_vmem = pl.BlockSpec(memory_space=pltpu.VMEM)
    return pl.pallas_call(
        own_image_kernel,
        out_shape=jax.ShapeDtypeStruct((height, twice_y), jnp.bfloat16),
        in_specs=[pl.BlockSpec(memory_space=pltpu.SMEM), pl.BlockSpec(memory_space=pl.ANY), in_vmem, in_vmem],
        out_specs=pl.BlockSpec(memory_space=pl.ANY),
        scratch_shapes=[
            pltpu.VMEM((count, width_x, twice_y), jnp.float32),
            pltpu.VMEM((height, twice_y), jnp.bfloat16),
            pltpu.SemaphoreType.DMA((count,)),
            pltpu.SemaphoreType.DMA((count + 1,)),
        ],
        compiler_params=pltpu.CompilerParams(vmem_limit_bytes=OWN_VMEM),
        name="own_image",
    )(which, image, bins, lines)


def per_device(image, coil_maps, kdata, phase_bin, line_index):
    owners = lax.axis_size("phase")
    groups = lax.axis_size("coil")
    group = lax.axis_index("coil")
    me = lax.axis_index("phase").astype(jnp.int32)
    rows = kdata.shape[0]
    venc, ncoil, twice_x = kdata.shape[1], kdata.shape[3], kdata.shape[4]
    width_x = twice_x // 2
    width_y = image.shape[-1] // 2
    own_venc = venc // groups
    capacity = 2 * rows // owners
    slots = owners * capacity
    which = group.reshape(1).astype(jnp.int32)
    zero = jnp.zeros((), jnp.int32)

    mine = own_image(which, image, phase_bin.reshape(1, rows), line_index.reshape(1, rows), own_venc)
    prior = passed_along(mine, "phase", 1)
    later = passed_along(mine, "phase", -1)

    others = []
    for k in range(1, groups):
        part = lax.dynamic_slice_in_dim(kdata, (group + k) % groups * own_venc, own_venc, 1)
        others.append(passed_along(part, "coil", k))
    late_maps, *others = lax.optimization_barrier((coil_maps, *others))
    all_maps = [coil_maps] + [passed_along(late_maps, "coil", k) for k in range(1, groups)]

    bins = phase_bin[:, 0]
    key = jnp.broadcast_to(bins[:, None], (rows, ncoil)).reshape(1, rows * ncoil)
    (packed,) = pack(jnp.stack([which[0], zero]), kdata, key, owners, capacity, own_venc, [(0, slots, None)])
    first = lax.all_to_all(packed, "phase", split_axis=0, concat_axis=0, tiled=True)

    code, _ = lax.optimization_barrier((bins * width_y + line_index, mine))
    tail = own_venc * image.shape[2] * width_x

    def sent_along(near):
        row = near[tail].astype(jnp.int32)
        return row[:rows] * width_y + row[128:128 + rows]

    codes = [code, sent_along(prior)]
    codes += [passed_along(code, "phase", k) for k in range(2, owners - 1)] + [sent_along(later)]
    codes = jnp.stack(codes)
    hits = codes // width_y == me
    rank = jnp.cumsum(hits.astype(jnp.int32), axis=1) - 1
    chosen = (rank[:, None] == jnp.arange(capacity, dtype=jnp.int32)[:, None]) & hits[:, None]
    lines = jnp.sum(jnp.where(chosen, (codes % width_y + 1)[:, None], 0), axis=2) - 1

    waiting = []
    places = [(k, v) for k in (0, 1) for v in [None]] + [(k, v) for v in range(own_venc) for k in range(2, owners)]
    for other in others:
        pieces = [(k * capacity, capacity, v) for k, v in places]
        packed = pack(jnp.stack([zero, me]), other, key, owners, capacity, own_venc, pieces)
        waiting.append(dict(zip(places, packed)))

    def tables(lines):
        lines = lines.reshape(slots)
        etable = expansion_table(jnp.maximum(lines, 0), (lines >= 0).astype(jnp.float32), width_y)
        high, low = split(etable)
        return etable, jnp.concatenate([high, high, low], axis=0)

    senders = (me - jnp.arange(owners, dtype=jnp.int32)) % owners
    picked = (senders[:, None] == jnp.arange(owners, dtype=jnp.int32)[None, :]).astype(jnp.int32)
    etable, e_other = tables(lines)
    _, e_first = tables(jnp.sum(picked[:, :, None] * lines[None], axis=1))
    ktable = jnp.dot(etable.T, etable, precision=lax.Precision.HIGHEST)
    ktable = jnp.stack(split(ktable))
    ttable = jnp.asarray(np.concatenate(split_numpy(inverse_table(width_x)), axis=1))

    acc = model_part(which, image, all_maps[0], ktable, (prior, later), own_venc)
    for k in range(1, groups):
        acc = model_part(which, image, all_maps[k], ktable, (acc,), own_venc)
    arrived = []
    for pieces in waiting:
        late = [place for place in places if place[1] == own_venc - 1]
        held, acc = lax.optimization_barrier(([pieces[place] for place in late], acc))
        pieces.update(zip(late, held))
        moved = {
            place: (p if place[0] == 0 else passed_along(p, "phase", place[0]), place[1] is None)
            for place, p in pieces.items()
        }
        for v in range(own_venc):
            arrived.append([moved[k, None] for k in (0, 1)] + [moved[k, v] for k in range(2, owners)])
    acc = data_part([(first, True)], all_maps[0], ttable, e_first, acc, (0, own_venc))
    for k, blocks in enumerate(arrived):
        acc = data_part(blocks, all_maps[1 + k // own_venc], ttable, e_other, acc, (k % own_venc, 1))
    return acc[None]


def solution(mesh):
    in_specs = (
        P("phase", None, "slab", None, None),
        P("slab", "coil", None, None),
        P("phase", None, "slab", "coil", None),
        P("phase", None),
        P("phase"),
    )
    out_specs = P("phase", "coil", "slab", None, None)
    return jax.shard_map(
        per_device, mesh=mesh, in_specs=in_specs, out_specs=out_specs, check_vma=False
    )
```

```python
import functools
import math

import jax
import jax.numpy as jnp
import ml_dtypes
import numpy as np
from jax import lax
from jax.experimental import pallas as pl
from jax.experimental.pallas import tpu as pltpu
from jax.sharding import PartitionSpec as P


MODEL_VMEM, DATA_VMEM, PACK_VMEM, OWN_VMEM = 20 << 20, 24 << 20, 16 << 20, 60 << 20


def passed_along(x, axis, by):
    devices = lax.axis_size(axis)
    return lax.ppermute(x, axis, [(i, (i + by) % devices) for i in range(devices)])


def split_numpy(table):
    high = table.astype(np.float32).astype(ml_dtypes.bfloat16)
    low = (table - high.astype(np.float64)).astype(np.float32).astype(ml_dtypes.bfloat16)
    return high, low


def inverse_table(count):
    steps = np.arange(count)
    angles = 2.0 * np.pi / count * (steps[:, None] * steps[None, :] % count)
    real_part = np.cos(angles) / math.sqrt(count)
    imag_part = np.sin(angles) / math.sqrt(count)
    return np.block([[real_part, -imag_part], [imag_part, real_part]])


def split(x):
    high = lax.reduce_precision(x, 8, 7)
    return high.astype(jnp.bfloat16), (x - high).astype(jnp.bfloat16)


def split_in_kernel(x):
    high = x.astype(jnp.bfloat16)
    return high, (x - high.astype(jnp.float32)).astype(jnp.bfloat16)


def expansion_table(lines, valid, count):
    steps = jnp.arange(count, dtype=jnp.int32)
    turns = lines[:, None] * steps[None, :] % count
    angles = 2.0 * math.pi / count * turns.astype(jnp.float32)
    factor = valid[:, None] / math.sqrt(count)
    real_part = jnp.cos(angles) * factor
    imag_part = jnp.sin(angles) * factor
    upper = jnp.concatenate([real_part, imag_part], axis=1)
    lower = jnp.concatenate([-imag_part, real_part], axis=1)
    return jnp.concatenate([upper, lower], axis=0)


def dot(a, b):
    return lax.dot_general(a, b, (((1,), (0,)), ((), ())), preferred_element_type=jnp.float32)


def dot_t(a, b):
    return lax.dot_general(a, b, (((1,), (1,)), ((), ())), preferred_element_type=jnp.float32)


def model_kernel(first, _, image_ref, maps_ref, k_ref, *rest):
    if first:
        near_refs, out_ref = rest[:-1], rest[-1]
    else:
        acc_ref, out_ref = rest
    own_venc, rows, twice_y = out_ref.shape[0], out_ref.shape[2], out_ref.shape[3]
    ncoil = maps_ref.shape[1]
    y = twice_y // 2
    for v in range(own_venc):
        x_re = image_ref[0, v, 0, :, :y]
        x_im = image_ref[0, v, 0, :, y:]
        parts = []
        for c in range(ncoil):
            s_re = maps_ref[0, c, :, :y].astype(jnp.float32)
            s_im = maps_ref[0, c, :, y:].astype(jnp.float32)
            parts.append(
                jnp.concatenate([s_re * x_re - s_im * x_im, s_re * x_im + s_im * x_re], axis=1)
            )
        high, low = split_in_kernel(jnp.concatenate(parts, axis=0))
        grid = dot(high, k_ref[0]) + dot(low, k_ref[0]) + dot(high, k_ref[1])
        if first:
            near = near_refs[2 * v][...].astype(jnp.float32) + near_refs[2 * v + 1][...].astype(jnp.float32)
            sum_re = x_re - 0.5 * near[:, :y]
            sum_im = x_im - 0.5 * near[:, y:]
        else:
            sum_re, sum_im = acc_ref[v, 0, :, :y], acc_ref[v, 0, :, y:]
        for c in range(ncoil):
            s_re = maps_ref[0, c, :, :y].astype(jnp.float32)
            s_im = maps_ref[0, c, :, y:].astype(jnp.float32)
            g_re = grid[c * rows:(c + 1) * rows, :y]
            g_im = grid[c * rows:(c + 1) * rows, y:]
            sum_re = sum_re + s_re * g_re + s_im * g_im
            sum_im = sum_im + s_re * g_im - s_im * g_re
        out_ref[v, 0, :, :y] = sum_re
        out_ref[v, 0, :, y:] = sum_im


def model_part(which, image, maps, ktable, before, own_venc):
    _, _, slabs, width_x, twice_y = image.shape
    ncoil = maps.shape[1]
    block = 64
    out_spec = pl.BlockSpec((own_venc, 1, block, twice_y), lambda s, i, w: (0, s, i, 0))
    in_specs = [
        pl.BlockSpec((1, own_venc, 1, block, twice_y), lambda s, i, w: (0, w[0], s, i, 0)),
        pl.BlockSpec((1, ncoil, block, twice_y), lambda s, i, w: (s, 0, i, 0)),
        pl.BlockSpec((2, twice_y, twice_y), lambda s, i, w: (0, 0, 0)),
    ]
    if len(before) == 2:
        steps = width_x // block
        near_specs = [
            pl.BlockSpec((block, twice_y), lambda s, i, w, v=v: ((v * slabs + s) * steps + i, 0))
            for v in range(own_venc)
        ]
        in_specs += [spec for spec in near_specs for _ in before]
        args = list(before) * own_venc
    else:
        in_specs.append(out_spec)
        args = list(before)
    products = own_venc * slabs * ncoil * width_x
    return pl.pallas_call(
        functools.partial(model_kernel, len(before) == 2),
        out_shape=jax.ShapeDtypeStruct((own_venc, slabs, width_x, twice_y), jnp.float32),
        grid_spec=pltpu.PrefetchScalarGridSpec(
            num_scalar_prefetch=1, grid=(slabs, width_x // block), in_specs=in_specs, out_specs=out_spec
        ),
        compiler_params=pltpu.CompilerParams(vmem_limit_bytes=MODEL_VMEM),
        cost_estimate=pl.CostEstimate(
            flops=6 * products * twice_y * twice_y, bytes_accessed=8 << 20, transcendentals=0
        ),
        name="model_part",
    )(which, image, maps, ktable, *args)


def pack_kernel(owners, capacity, pieces, at_ref, rows_ref, key_ref, *rest):
    outs, place_ref = rest[:-1], rest[-1]
    ncoil, twice_x = rows_ref.shape[3], rows_ref.shape[4]
    wide = key_ref.shape[1]
    total = owners * capacity

    @pl.when(pl.program_id(0) == 0)
    def _():
        key = key_ref[...] - at_ref[1]
        key = jnp.where(key < 0, key + owners, key)
        owner = lax.broadcasted_iota(jnp.int32, (-(-owners // 8) * 8, wide), 0)
        hits = owner == key
        i = lax.broadcasted_iota(jnp.int32, (wide, wide), 0)
        j = lax.broadcasted_iota(jnp.int32, (wide, wide), 1)
        earlier = ((i // ncoil < j // ncoil) & (i % ncoil == 0)).astype(jnp.bfloat16)
        before = dot(hits.astype(jnp.bfloat16), earlier)
        rank = jnp.sum(jnp.where(hits, before, 0.0), axis=0, keepdims=True).astype(jnp.int32)
        target = key * capacity + rank
        a = lax.broadcasted_iota(jnp.int32, (ncoil * total, wide), 0)
        b = lax.broadcasted_iota(jnp.int32, (ncoil * total, wide), 1)
        place_ref[...] = ((a % total == target) & (a // total == b % ncoil)).astype(jnp.bfloat16)

    own_venc = rows_ref.shape[1]
    for v in range(own_venc):
        packed = dot(place_ref[...], rows_ref[:, v, 0].reshape(wide, twice_x)).astype(jnp.bfloat16)
        for (first, height, only), out_ref in zip(pieces, outs):
            if only is None or only == v:
                for c in range(ncoil):
                    lane = (c if only == v else v * ncoil + c) * twice_x
                    start = c * total + first
                    out_ref[:, lane:lane + twice_x] = packed[start:start + height]


def pack(at, rows, key, owners, capacity, own_venc, pieces):
    count, _, slabs, ncoil, twice_x = rows.shape
    shapes = [(h, ncoil * twice_x * (own_venc if v is None else 1)) for _, h, v in pieces]
    return pl.pallas_call(
        functools.partial(pack_kernel, owners, capacity, pieces),
        out_shape=[jax.ShapeDtypeStruct((h, slabs * w), jnp.bfloat16) for h, w in shapes],
        grid_spec=pltpu.PrefetchScalarGridSpec(
            num_scalar_prefetch=1,
            grid=(slabs,),
            in_specs=[
                pl.BlockSpec((count, own_venc, 1, ncoil, twice_x), lambda s, w: (0, w[0], s, 0, 0)),
                pl.BlockSpec((1, count * ncoil), lambda s, w: (0, 0)),
            ],
            out_specs=[pl.BlockSpec(shape, lambda s, w: (0, s)) for shape in shapes],
            scratch_shapes=[pltpu.VMEM((ncoil * owners * capacity, count * ncoil), jnp.bfloat16)],
        ),
        compiler_params=pltpu.CompilerParams(vmem_limit_bytes=PACK_VMEM),
        name="pack",
    )(at, rows, key)


def data_kernel(count, *refs):
    rows_refs, (maps_ref, t_ref, e_ref, acc_ref, out_ref) = refs[:count], refs[count:]
    slots = e_ref.shape[0] // 6
    ncoil, x, twice_y = maps_ref.shape[1], maps_ref.shape[2], maps_ref.shape[3]
    y = twice_y // 2
    twice_x = 2 * x
    sum_re = acc_ref[0, 0, :, :y]
    sum_im = acc_ref[0, 0, :, y:]
    for first in range(0, ncoil, 4):
        pair = jnp.concatenate(
            [
                ref[:, c * twice_x:(c + 1) * twice_x]
                for c in range(first, first + 4)
                for ref in rows_refs
            ],
            axis=0,
        )
        along_x = dot_t(t_ref[...], jnp.concatenate([pair, pair], axis=1))
        lhs = jnp.concatenate(
            [
                jnp.concatenate(
                    [along_x[:x, i * slots:(i + 1) * slots], along_x[x:, i * slots:(i + 1) * slots]],
                    axis=1,
                )
                for i in range(4)
            ],
            axis=0,
        )
        high, low = split_in_kernel(lhs)
        grid = dot(jnp.concatenate([high, low, high], axis=1), e_ref[...])
        for i in range(4):
            s_re = maps_ref[0, first + i, :, :y].astype(jnp.float32)
            s_im = maps_ref[0, first + i, :, y:].astype(jnp.float32)
            g_re = grid[i * x:(i + 1) * x, :y]
            g_im = grid[i * x:(i + 1) * x, y:]
            sum_re = sum_re - (s_re * g_re + s_im * g_im)
            sum_im = sum_im - (s_re * g_im - s_im * g_re)
    out_ref[0, 0, :, :y] = sum_re
    out_ref[0, 0, :, y:] = sum_im


def data_part(rows, maps, ttable, etable, acc, encodings):
    capacity = rows[0][0].shape[0]
    slots = capacity * len(rows)
    own_venc = acc.shape[0]
    slabs, ncoil, width_x, twice_y = maps.shape
    twice_x = 2 * width_x
    first, count = encodings
    const = lambda s, v: (0, 0)
    frame = pl.BlockSpec((1, 1, width_x, twice_y), lambda s, v: (first + v, s, 0, 0))
    products = count * slabs * ncoil
    return pl.pallas_call(
        functools.partial(data_kernel, len(rows)),
        out_shape=jax.ShapeDtypeStruct(acc.shape, jnp.float32),
        grid=(slabs, count),
        in_specs=[
            pl.BlockSpec(
                (capacity, ncoil * twice_x), lambda s, v, every=every: (0, s * own_venc + first + v if every else s)
            )
            for _, every in rows
        ]
        + [
            pl.BlockSpec((1, ncoil, width_x, twice_y), lambda s, v: (s, 0, 0, 0)),
            pl.BlockSpec((twice_x, 2 * twice_x), const),
            pl.BlockSpec((6 * slots, twice_y), const),
            frame,
        ],
        out_specs=frame,
        input_output_aliases={len(rows) + 3: 0},
        compiler_params=pltpu.CompilerParams(vmem_limit_bytes=DATA_VMEM),
        cost_estimate=pl.CostEstimate(
            flops=products * (4 * slots * twice_x * twice_x + 12 * slots * width_x * twice_y),
            bytes_accessed=8 << 20,
            transcendentals=0,
        ),
        name="data_part",
    )(*[array for array, _ in rows], maps, ttable, etable, acc)


def own_image_kernel(which_ref, image_ref, bins_ref, lines_ref, out_ref, wide_ref, narrow_ref, in_sems, out_sems):
    count, width_x = wide_ref.shape[0], wide_ref.shape[1]
    slabs = image_ref.shape[2]
    own_venc = count // slabs
    rows = bins_ref.shape[1]
    first = which_ref[0] * own_venc
    fetches = [
        pltpu.make_async_copy(image_ref.at[0, first + i // slabs, i % slabs], wide_ref.at[i], in_sems.at[i])
        for i in range(count)
    ]
    for fetch in fetches:
        fetch.start()
    spans = [pl.ds(i * width_x, width_x) for i in range(count)] + [pl.ds(count * width_x, 16)]
    stores = [
        pltpu.make_async_copy(narrow_ref.at[span], out_ref.at[span], out_sems.at[i])
        for i, span in enumerate(spans)
    ]
    narrow_ref[spans[-1], :] = jnp.zeros((16, narrow_ref.shape[1]), jnp.bfloat16)
    for lane, values in ((0, bins_ref), (128, lines_ref)):
        block = jnp.broadcast_to(values[...].astype(jnp.float32), (16, rows))
        narrow_ref[spans[-1], lane:lane + rows] = block.astype(jnp.bfloat16)
    stores[-1].start()
    for i, (fetch, store) in enumerate(zip(fetches, stores)):
        fetch.wait()
        narrow_ref[spans[i], :] = wide_ref[i].astype(jnp.bfloat16)
        store.start()
    for store in stores:
        store.wait()


def own_image(which, image, bins, lines, own_venc):
    _, _, slabs, width_x, twice_y = image.shape
    count = own_venc * slabs
    height = count * width_x + 16
    in_vmem = pl.BlockSpec(memory_space=pltpu.VMEM)
    return pl.pallas_call(
        own_image_kernel,
        out_shape=jax.ShapeDtypeStruct((height, twice_y), jnp.bfloat16),
        in_specs=[pl.BlockSpec(memory_space=pltpu.SMEM), pl.BlockSpec(memory_space=pl.ANY), in_vmem, in_vmem],
        out_specs=pl.BlockSpec(memory_space=pl.ANY),
        scratch_shapes=[
            pltpu.VMEM((count, width_x, twice_y), jnp.float32),
            pltpu.VMEM((height, twice_y), jnp.bfloat16),
            pltpu.SemaphoreType.DMA((count,)),
            pltpu.SemaphoreType.DMA((count + 1,)),
        ],
        compiler_params=pltpu.CompilerParams(vmem_limit_bytes=OWN_VMEM),
        name="own_image",
    )(which, image, bins, lines)


def per_device(image, coil_maps, kdata, phase_bin, line_index):
    owners = lax.axis_size("phase")
    groups = lax.axis_size("coil")
    group = lax.axis_index("coil")
    me = lax.axis_index("phase").astype(jnp.int32)
    rows = kdata.shape[0]
    venc, ncoil, twice_x = kdata.shape[1], kdata.shape[3], kdata.shape[4]
    width_x = twice_x // 2
    width_y = image.shape[-1] // 2
    own_venc = venc // groups
    capacity = 2 * rows // owners
    slots = owners * capacity
    which = group.reshape(1).astype(jnp.int32)
    zero = jnp.zeros((), jnp.int32)

    mine = own_image(which, image, phase_bin.reshape(1, rows), line_index.reshape(1, rows), own_venc)
    prior = passed_along(mine, "phase", 1)
    later = passed_along(mine, "phase", -1)

    others = []
    for k in range(1, groups):
        part = lax.dynamic_slice_in_dim(kdata, (group + k) % groups * own_venc, own_venc, 1)
        others.append(passed_along(part, "coil", k))
    late_maps, *others = lax.optimization_barrier((coil_maps, *others))
    all_maps = [coil_maps] + [passed_along(late_maps, "coil", k) for k in range(1, groups)]

    bins = phase_bin[:, 0]
    key = jnp.broadcast_to(bins[:, None], (rows, ncoil)).reshape(1, rows * ncoil)
    (packed,) = pack(jnp.stack([which[0], zero]), kdata, key, owners, capacity, own_venc, [(0, slots, None)])
    first = lax.all_to_all(packed, "phase", split_axis=0, concat_axis=0, tiled=True)

    code, _ = lax.optimization_barrier((bins * width_y + line_index, mine))
    tail = own_venc * image.shape[2] * width_x

    def sent_along(near):
        row = near[tail].astype(jnp.int32)
        return row[:rows] * width_y + row[128:128 + rows]

    codes = [code, sent_along(prior)]
    codes += [passed_along(code, "phase", k) for k in range(2, owners - 1)] + [sent_along(later)]
    codes = jnp.stack(codes)
    hits = codes // width_y == me
    rank = jnp.cumsum(hits.astype(jnp.int32), axis=1) - 1
    chosen = (rank[:, None] == jnp.arange(capacity, dtype=jnp.int32)[:, None]) & hits[:, None]
    lines = jnp.sum(jnp.where(chosen, (codes % width_y + 1)[:, None], 0), axis=2) - 1

    waiting = []
    places = [(0, None)] + [(k, v) for v in range(own_venc) for k in range(1, owners)]
    for other in others:
        pieces = [(k * capacity, capacity, v) for k, v in places]
        packed = pack(jnp.stack([zero, me]), other, key, owners, capacity, own_venc, pieces)
        waiting.append(dict(zip(places, packed)))

    def tables(lines):
        lines = lines.reshape(slots)
        etable = expansion_table(jnp.maximum(lines, 0), (lines >= 0).astype(jnp.float32), width_y)
        high, low = split(etable)
        return etable, jnp.concatenate([high, high, low], axis=0)

    senders = (me - jnp.arange(owners, dtype=jnp.int32)) % owners
    picked = (senders[:, None] == jnp.arange(owners, dtype=jnp.int32)[None, :]).astype(jnp.int32)
    etable, e_other = tables(lines)
    _, e_first = tables(jnp.sum(picked[:, :, None] * lines[None], axis=1))
    ktable = jnp.dot(etable.T, etable, precision=lax.Precision.HIGHEST)
    ktable = jnp.stack(split(ktable))
    ttable = jnp.asarray(np.concatenate(split_numpy(inverse_table(width_x)), axis=1))

    acc = model_part(which, image, all_maps[0], ktable, (prior, later), own_venc)
    for k in range(1, groups):
        acc = model_part(which, image, all_maps[k], ktable, (acc,), own_venc)
    def held(pieces, late, acc):
        parts, acc = lax.optimization_barrier(([pieces[place] for place in late], acc))
        moved = {place: (passed_along(p, "phase", place[0]), False) for place, p in zip(late, parts)}
        return moved, acc

    final = own_venc - 1
    moved = []
    for pieces in waiting:
        now = {
            place: (p if place[0] == 0 else passed_along(p, "phase", place[0]), place[1] is None)
            for place, p in pieces.items()
            if place[1] != final
        }
        late, acc = held(pieces, [(k, final) for k in range(2, owners)], acc)
        moved.append({**now, **late})
    for pieces, now in zip(waiting, moved):
        late, first = held(pieces, [(1, final)], first)
        now.update(late)
    acc = data_part([(first, True)], all_maps[0], ttable, e_first, acc, (0, own_venc))
    for now, maps in zip(moved, all_maps[1:]):
        for v in range(own_venc):
            blocks = [now[0, None]] + [now[k, v] for k in range(1, owners)]
            acc = data_part(blocks, maps, ttable, e_other, acc, (v, 1))
    return acc[None]


def solution(mesh):
    in_specs = (
        P("phase", None, "slab", None, None),
        P("slab", "coil", None, None),
        P("phase", None, "slab", "coil", None),
        P("phase", None),
        P("phase"),
    )
    out_specs = P("phase", "coil", "slab", None, None)
    return jax.shard_map(
        per_device, mesh=mesh, in_specs=in_specs, out_specs=out_specs, check_vma=False
    )
```
